512 devices in a mesh: mode: 8 (over x, z_lo), space: 64 (over y, z_hi, core).
Axes of the slice: x: 4, y: 8, z: 8 (z_hi: 4, z_lo: 2; z = z_hi * 2 + z_lo), core: 2. Of those that a mesh axis runs over, the one named last changes fastest.
Arguments:
- mode_fields: bfloat16 [512, 2, 256, 256], P('mode', None, 'space'), may hold values from -6 to 6
- metric: float32 [3, 256, 256], P(None, 'space'), may hold values from 0.5 to 2
- plan: int32 [4, 2], replicated, may hold values from 0 to 7, as said below
Outputs:
- tensor: float32 [4096, 512], P('space', 'mode')
The draws below stay inside these ranges and needn't reach their ends.
Inputs may be any that keep to these rules, and one draw needn't show every extreme that they name: `plan`: rows 0 and 1 name the advecting blocks, rows 2 and 3 the advected blocks: column 0 a mode group, column 1 a half of its modes (0 or 1). Blocks may repeat.
All inputs are finite; a program needn't handle non-finite values.
Results may differ from the reference program's by a relative error of at most 0.0041.
Values may be sent and summed in bfloat16 or wider, within the bound.
No kernel may reach another device: no remote copies, remote signals or barrier semaphores. Data moves between devices by JAX's collectives and lax.ppermute only.
A program may use at most 64 MiB of HBM per device.

```python
import math
import jax
import jax.numpy as jnp
from jax import lax

MODE_DEV = 64
MODES = 512
BLOCK = 32
NY = 256
NX = 256
N_MODE = 8


def draw_plan(key, part):
    first_key, second_key, third_key, fourth_key = jax.random.split(jax.random.fold_in(key, 17), 4)
    owners = jax.random.randint(first_key, (4,), 0, N_MODE)
    halves = jax.random.randint(second_key, (4,), 0, 2)
    top_slot = jax.random.randint(third_key, (), 0, 4)
    low_slot = jax.random.randint(fourth_key, (), 0, 4)
    places = jnp.arange(4)
    owners = jnp.where(places == top_slot, N_MODE - 1, owners)
    halves = jnp.where(places == low_slot, 0, halves)
    return jnp.stack([owners, halves], axis=1).astype(jnp.int32)


def block_scale(rng, shape, pieces, least, largest):
    gain = 1.0
    for position, blocks in pieces:
        steps = jax.random.uniform(jax.random.fold_in(jax.random.fold_in(rng, 6), position), (blocks,), jnp.float32, least / len(pieces), largest / len(pieces))
        gain = gain * jnp.repeat(jnp.exp(steps), shape[position] // blocks).reshape((-1,) + (1,) * (len(shape) - 1 - position))
    return gain


def scatter_about(key, shape, deviation, most, cuts=(), kind=jnp.bfloat16):
    array = jax.random.normal(key, shape, jnp.float32) * deviation
    if len(cuts) > 0:
        array = block_scale(key, shape, cuts, -0.22, 0.18) * array
    return jnp.clip(array, min=-most, max=most).astype(kind)


def setup_inputs(seed: int = 0) -> dict:
    splits = jax.random.split(jax.random.key(seed), 4)
    mode_fields = scatter_about(splits[0], (MODES, 2, NX, NY), 1.0, 6.0, ((0, 8), (2, 64)))
    metric = jnp.clip(jnp.exp(math.log(2.0) - 1.3862944 * jax.random.uniform(splits[1], (3, NX, NY), jnp.float32) ** block_scale(splits[1], (3, NX, NY), ((1, 64),), -0.2, 0.2)), 0.5, 2.0)
    plan = draw_plan(jax.random.fold_in(splits[3], 71), 0)
    return {"mode_fields": mode_fields, "metric": metric, "plan": plan}


def stencil(padded, metric):
    widened = padded.astype(jnp.float32)
    along_x = (widened[:, :, 2:, :] - widened[:, :, :-2, :]) * metric[0]
    interior = jnp.pad(widened[:, :, 1:-1, :], ((0, 0), (0, 0), (0, 0), (1, 1)))
    along_y = (interior[:, :, :, 2:] - interior[:, :, :, :-2]) * metric[1]
    return jnp.stack((along_x, along_y), axis=1).astype(jnp.bfloat16)


def advect(column, slopes, weight):
    widened = column.astype(jnp.float32)
    mixed = widened[0] * slopes[:, 0].astype(jnp.float32) + widened[1] * slopes[:, 1].astype(jnp.float32)
    return (mixed * weight).astype(jnp.bfloat16).reshape(slopes.shape[0], -1)


def reference(mode_fields, metric, plan):
    def own_block(source_row):
        first_row = plan[source_row, 0] * MODE_DEV + plan[source_row, 1] * BLOCK
        return lax.dynamic_slice_in_dim(mode_fields, first_row.astype(jnp.int32), BLOCK, 0)

    movers = jnp.concatenate([own_block(0), own_block(1)], axis=0)
    carried = jnp.concatenate([own_block(2), own_block(3)], axis=0)
    padded = jnp.pad(carried, ((0, 0), (0, 0), (1, 1), (0, 0)))
    slopes = stencil(padded, metric)
    test_rows = mode_fields.reshape(MODES, -1)

    def project(column):
        advected_field = advect(column, slopes, metric[2])
        return lax.dot_general(advected_field, test_rows, (((1,), (1,)), ((), ())), preferred_element_type=jnp.float32)

    blocks = lax.map(project, movers)
    return blocks.reshape(-1, MODES) * (float(NX * NY) ** -0.5)
```

```python
import jax
import jax.numpy as jnp
from jax import lax
from jax.experimental import pallas as pl
from jax.experimental.pallas import tpu as pltpu
from jax.sharding import Mesh, PartitionSpec as P

MODE = ("x", "zl")
SPACE = ("y", "zh", "c")
JB = 8


def kernel(c_ref, metric_ref, recv_ref, test_ref, out_ref, s_ref, wm_ref, phi_ref, f_ref, *, send):
    groups = recv_ref.shape[0]
    n = groups * recv_ref.shape[2]
    ny = recv_ref.shape[3]
    f32 = jnp.float32

    def row(index):
        return recv_ref[:, index].astype(f32).reshape(n, ny)

    @pl.when(pl.program_id(0) == 0)
    def _():
        lane = lax.broadcasted_iota(jnp.int32, (n, ny), 1)
        for c in range(2):
            for r in range(4):
                low = row(16 + c) if r == 0 else row(8 + 4 * c + r - 1)
                high = row(18 + c) if r == 3 else row(8 + 4 * c + r + 1)
                mid = row(8 + 4 * c + r)
                along_x = (high - low) * metric_ref[0, pl.ds(r, 1), :]
                after = jnp.where(lane == ny - 1, 0.0, pltpu.roll(mid, ny - 1, 1))
                before = jnp.where(lane == 0, 0.0, pltpu.roll(mid, 1, 1))
                along_y = (after - before) * metric_ref[1, pl.ds(r, 1), :]
                s_ref[0, 4 * c + r] = along_x.astype(jnp.bfloat16).astype(f32)
                s_ref[1, 4 * c + r] = along_y.astype(jnp.bfloat16).astype(f32)
                wm_ref[4 * c + r] = row(4 * c + r) * metric_ref[2, pl.ds(r, 1), :]
                phi_ref[:, pl.ds((4 * c + r) * ny, ny)] = test_ref[:, 4 * c + r].reshape(n, ny)

    parity = 1 - c_ref[0] if send else c_ref[0]
    base = pl.program_id(0) * (2 * JB) + parity
    for cr in range(8):
        r = cr % 4
        s0 = s_ref[0, cr]
        s1 = s_ref[1, cr]
        for b in range(JB):
            j = base + 2 * b
            field = wm_ref[r, pl.ds(j, 1), :] * s0 + wm_ref[4 + r, pl.ds(j, 1), :] * s1
            f_ref[pl.ds(b * n, n), pl.ds(cr * ny, ny)] = field.astype(jnp.bfloat16)
    res = lax.dot_general(f_ref[...], phi_ref[...], (((1,), (1,)), ((), ())), preferred_element_type=f32)
    res = res.reshape(JB, n, n)
    out_ref[...] = jnp.concatenate([res[:, : n // 2], res[:, n // 2 :]], axis=2)


def project(core, metric, recv, test, send):
    groups, _, m, ny = recv.shape
    n = groups * m
    movers = n // 2
    return pl.pallas_call(
        lambda *refs: kernel(*refs, send=send),
        grid=(movers // JB,),
        in_specs=[
            pl.BlockSpec(memory_space=pltpu.SMEM),
            pl.BlockSpec(metric.shape, lambda i: (0, 0, 0)),
            pl.BlockSpec(recv.shape, lambda i: (0, 0, 0, 0)),
            pl.BlockSpec(test.shape, lambda i: (0, 0, 0, 0)),
        ],
        out_specs=pl.BlockSpec((JB, n // 2, 2 * n), lambda i: (i, 0, 0)),
        out_shape=jax.ShapeDtypeStruct((movers, n // 2, 2 * n), jnp.float32),
        scratch_shapes=[
            pltpu.VMEM((2, 8, n, ny), jnp.float32),
            pltpu.VMEM((8, n, ny), jnp.float32),
            pltpu.VMEM((n, 8 * ny), jnp.bfloat16),
            pltpu.VMEM((JB * n, 8 * ny), jnp.bfloat16),
        ],
        compiler_params=pltpu.CompilerParams(dimension_semantics=("arbitrary",)),
        name="project_send" if send else "project_keep",
    )(core, metric, recv, test)


def body(mode_fields, metric, plan):
    n = mode_fields.shape[0]
    ny = mode_fields.shape[3]
    groups = lax.axis_size(MODE)
    m = n // groups
    half = groups // 2
    fields = mode_fields.reshape(groups, m, 2, 4, ny).transpose(0, 2, 3, 1, 4).reshape(groups, 8, m, ny)

    def candidates(row):
        return lax.dynamic_slice_in_dim(fields, plan[row, 1] * half, half, 0)

    movers = jnp.concatenate([candidates(0), candidates(1)], axis=0)
    carried = jnp.concatenate([candidates(2), candidates(3)], axis=0)
    pieces = lax.all_to_all(
        jnp.concatenate([movers, carried], axis=1), MODE, 0, 0, tiled=True
    )
    block = lax.axis_index(MODE) // half
    mover = lax.dynamic_index_in_dim(pieces[:, :8], plan[block, 0], 0, keepdims=False)
    moved = lax.dynamic_index_in_dim(pieces[:, 8:], plan[2 + block, 0], 0, keepdims=False)
    count = lax.axis_size(SPACE)
    forward = [(i, i + 1) for i in range(count - 1)]
    backward = [(i + 1, i) for i in range(count - 1)]
    by_row = moved.reshape(2, 4, m, ny)
    low = lax.ppermute(by_row[:, 3], SPACE, forward)
    high = lax.ppermute(by_row[:, 0], SPACE, backward)
    piece = jnp.concatenate([mover, moved, low, high], axis=0)
    recv = lax.all_to_all(
        jnp.broadcast_to(piece[None], (groups,) + piece.shape), MODE, 0, 0, tiled=True
    )
    core = lax.axis_index("c").astype(jnp.int32).reshape(1)
    sent = project(core, metric, recv, fields, True)
    other = lax.ppermute(sent, "c", [(0, 1), (1, 0)])
    kept = project(core, metric, recv, fields, False)
    shares = lax.all_to_all(kept + other, ("y", "zh"), 0, 0, tiled=True)
    norm_factor = float(4 * count * ny) ** (-0.5)
    total = jnp.sum(shares, axis=0) * norm_factor
    return jnp.concatenate([total[:, :n], total[:, n:]], axis=0)


def solution(mesh):
    fine = Mesh(mesh.devices.reshape(4, 2, 8, 4, 2), ("x", "zl", "y", "zh", "c"))
    return jax.shard_map(
        body,
        mesh=fine,
        in_specs=(P(MODE, None, SPACE, None), P(None, SPACE, None), P()),
        out_specs=P(SPACE, MODE),
        check_vma=False,
    )
```

```python
import jax
import jax.numpy as jnp
from jax import lax
from jax.experimental import pallas as pl
from jax.experimental.pallas import tpu as pltpu
from jax.sharding import Mesh, PartitionSpec as P

MODE = ("x", "zl")
SPACE = ("y", "zh", "c")
JB = 8
CHUNKS = 2
LIMIT = 16 * 2**20
SMEM = pl.BlockSpec(memory_space=pltpu.SMEM)
ANY = pl.BlockSpec(memory_space=pl.ANY)


def run_copies(pairs, sems):
    copies = [pltpu.make_async_copy(src, dst, sems.at[i]) for i, (src, dst) in enumerate(pairs)]
    for copy in copies:
        copy.start()
    for copy in copies:
        copy.wait()


def pack_kernel(plan_ref, fields_ref, low_ref, high_ref, out_ref, sems):
    half = fields_ref.shape[0] // 2
    pairs = []
    for b in range(2):
        here = pl.ds(b * half, half)
        mover = pl.ds(plan_ref[b, 1] * half, half)
        moved = pl.ds(plan_ref[2 + b, 1] * half, half)
        pairs += [
            (fields_ref.at[mover], out_ref.at[here, 0:8]),
            (fields_ref.at[moved], out_ref.at[here, 8:16]),
            (low_ref.at[moved], out_ref.at[here, 16:18]),
            (high_ref.at[moved], out_ref.at[here, 18:20]),
        ]
    run_copies(pairs, sems)


def pack(plan, fields, low, high):
    groups, _, m, ny = fields.shape
    return pl.pallas_call(
        pack_kernel,
        in_specs=[SMEM, ANY, ANY, ANY],
        out_specs=ANY,
        out_shape=jax.ShapeDtypeStruct((groups, 20, m, ny), fields.dtype),
        scratch_shapes=[pltpu.SemaphoreType.DMA((8,))],
        compiler_params=pltpu.CompilerParams(vmem_limit_bytes=LIMIT),
        name="pack",
    )(plan, fields, low, high)


def choose_kernel(plan_ref, place_ref, pieces_ref, out_ref, sems):
    groups = pieces_ref.shape[0]
    block = place_ref[0] // (groups // 2)
    mover = plan_ref[block, 0]
    moved = plan_ref[2 + block, 0]
    pairs = []
    for g in range(groups):
        pairs += [
            (pieces_ref.at[mover, 0:8], out_ref.at[g, 0:8]),
            (pieces_ref.at[moved, 8:20], out_ref.at[g, 8:20]),
        ]
    run_copies(pairs, sems)


def choose(plan, place, pieces):
    return pl.pallas_call(
        choose_kernel,
        in_specs=[SMEM, SMEM, ANY],
        out_specs=ANY,
        out_shape=jax.ShapeDtypeStruct(pieces.shape, pieces.dtype),
        scratch_shapes=[pltpu.SemaphoreType.DMA((16,))],
        compiler_params=pltpu.CompilerParams(vmem_limit_bytes=LIMIT),
        name="choose",
    )(plan, place, pieces)


def kernel(
    c_ref, metric_any, recv_any, test_any, out_ref,
    metric_ref, recv_ref, test_ref, s_ref, wm_ref, phi_ref, f_ref, sems, *, send, chunk
):
    groups, _, m, ny = recv_ref.shape
    n = groups * m
    part = groups // CHUNKS
    k = n // CHUNKS
    f32 = jnp.float32

    def row(index):
        return recv_ref[chunk * part : (chunk + 1) * part, index].astype(f32).reshape(k, ny)

    @pl.when(pl.program_id(0) == 0)
    def _():
        run_copies([(metric_any, metric_ref), (recv_any, recv_ref), (test_any, test_ref)], sems)
        lane = lax.broadcasted_iota(jnp.int32, (k, ny), 1)
        for c in range(2):
            for r in range(4):
                low = row(16 + c) if r == 0 else row(8 + 4 * c + r - 1)
                high = row(18 + c) if r == 3 else row(8 + 4 * c + r + 1)
                mid = row(8 + 4 * c + r)
                along_x = (high - low) * metric_ref[0, pl.ds(r, 1), :]
                after = jnp.where(lane == ny - 1, 0.0, pltpu.roll(mid, ny - 1, 1))
                before = jnp.where(lane == 0, 0.0, pltpu.roll(mid, 1, 1))
                along_y = (after - before) * metric_ref[1, pl.ds(r, 1), :]
                s_ref[0, 4 * c + r] = along_x.astype(jnp.bfloat16).astype(f32)
                s_ref[1, 4 * c + r] = along_y.astype(jnp.bfloat16).astype(f32)
                mover = recv_ref[:, 4 * c + r].astype(f32).reshape(n, ny)
                wm_ref[4 * c + r] = mover * metric_ref[2, pl.ds(r, 1), :]
                phi_ref[:, pl.ds((4 * c + r) * ny, ny)] = test_ref[:, 4 * c + r].reshape(n, ny)

    parity = 1 - c_ref[0] if send else c_ref[0]
    base = pl.program_id(0) * (2 * JB) + parity
    for cr in range(8):
        r = cr % 4
        s0 = s_ref[0, cr]
        s1 = s_ref[1, cr]
        for b in range(JB):
            j = base + 2 * b
            field = wm_ref[r, pl.ds(j, 1), :] * s0 + wm_ref[4 + r, pl.ds(j, 1), :] * s1
            f_ref[pl.ds(b * k, k), pl.ds(cr * ny, ny)] = field.astype(jnp.bfloat16)
    res = lax.dot_general(f_ref[...], phi_ref[...], (((1,), (1,)), ((), ())), preferred_element_type=f32)
    res = res.reshape(JB, k, n)
    out_ref[...] = jnp.concatenate([res[:, : k // 2], res[:, k // 2 :]], axis=2)


def project(core, metric, recv, test, send, chunk):
    groups, _, m, ny = recv.shape
    n = groups * m
    movers = n // 2
    k = n // CHUNKS
    return pl.pallas_call(
        lambda *refs: kernel(*refs, send=send, chunk=chunk),
        grid=(movers // JB,),
        in_specs=[SMEM, ANY, ANY, ANY],
        out_specs=pl.BlockSpec((JB, k // 2, 2 * n), lambda i: (i, 0, 0)),
        out_shape=jax.ShapeDtypeStruct((movers, k // 2, 2 * n), jnp.float32),
        scratch_shapes=[
            pltpu.VMEM(metric.shape, metric.dtype),
            pltpu.VMEM(recv.shape, recv.dtype),
            pltpu.VMEM(test.shape, test.dtype),
            pltpu.VMEM((2, 8, k, ny), jnp.float32),
            pltpu.VMEM((8, n, ny), jnp.float32),
            pltpu.VMEM((n, 8 * ny), jnp.bfloat16),
            pltpu.VMEM((JB * k, 8 * ny), jnp.bfloat16),
            pltpu.SemaphoreType.DMA((3,)),
        ],
        compiler_params=pltpu.CompilerParams(dimension_semantics=("arbitrary",), vmem_limit_bytes=LIMIT),
        name=f"project_{chunk}_{'send' if send else 'keep'}",
    )(core, metric, recv, test)


def body(mode_fields, metric, plan):
    n = mode_fields.shape[0]
    ny = mode_fields.shape[3]
    groups = lax.axis_size(MODE)
    m = n // groups
    by_row = mode_fields.reshape(groups, m, 2, 4, ny).transpose(0, 2, 3, 1, 4)
    fields = by_row.reshape(groups, 8, m, ny)
    count = lax.axis_size(SPACE)
    forward = [(i, i + 1) for i in range(count - 1)]
    backward = [(i + 1, i) for i in range(count - 1)]
    low = lax.ppermute(by_row[:, :, 3], SPACE, forward)
    high = lax.ppermute(by_row[:, :, 0], SPACE, backward)
    pieces = lax.all_to_all(pack(plan, fields, low, high), MODE, 0, 0, tiled=True)
    place = lax.axis_index(MODE).astype(jnp.int32).reshape(1)
    recv = lax.all_to_all(choose(plan, place, pieces), MODE, 0, 0, tiled=True)
    core = lax.axis_index("c").astype(jnp.int32).reshape(1)
    norm_factor = float(4 * count * ny) ** (-0.5)
    shares = []
    for chunk in range(CHUNKS):
        sent = project(core, metric, recv, fields, True, chunk)
        other = lax.ppermute(sent, "c", [(0, 1), (1, 0)])
        kept = project(core, metric, recv, fields, False, chunk)
        shares.append(lax.all_to_all(kept + other, ("y", "zh"), 0, 0, tiled=True))
    rows = []
    for share in shares:
        total = jnp.sum(share, axis=0) * norm_factor
        rows += [total[:, :n], total[:, n:]]
    return jnp.concatenate(rows, axis=0)


def solution(mesh):
    fine = Mesh(mesh.devices.reshape(4, 2, 8, 4, 2), ("x", "zl", "y", "zh", "c"))
    return jax.shard_map(
        body,
        mesh=fine,
        in_specs=(P(MODE, None, SPACE, None), P(None, SPACE, None), P()),
        out_specs=P(SPACE, MODE),
        check_vma=False,
    )
```

```python
import jax
import jax.numpy as jnp
from jax import lax
from jax.experimental import pallas as pl
from jax.experimental.pallas import tpu as pltpu
from jax.sharding import Mesh, PartitionSpec as P

MODE = ("x", "zl")
SPACE = ("y", "zh", "c")
JB = 8
LIMIT = 16 * 2**20
SMEM = pl.BlockSpec(memory_space=pltpu.SMEM)
ANY = pl.BlockSpec(memory_space=pl.ANY)


def run_copies(pairs, sems):
    copies = [pltpu.make_async_copy(src, dst, sems.at[i]) for i, (src, dst) in enumerate(pairs)]
    for copy in copies:
        copy.start()
    for copy in copies:
        copy.wait()


def pack_kernel(plan_ref, fields_ref, out_ref, sems):
    half = fields_ref.shape[0] // 2
    pairs = []
    for b in range(2):
        here = pl.ds(b * half, half)
        mover = pl.ds(plan_ref[b, 1] * half, half)
        moved = pl.ds(plan_ref[2 + b, 1] * half, half)
        pairs += [
            (fields_ref.at[mover], out_ref.at[here, 0:8]),
            (fields_ref.at[moved], out_ref.at[here, 8:16]),
        ]
    run_copies(pairs, sems)


def pack(plan, fields):
    groups, _, m, ny = fields.shape
    return pl.pallas_call(
        pack_kernel,
        in_specs=[SMEM, ANY],
        out_specs=ANY,
        out_shape=jax.ShapeDtypeStruct((groups, 16, m, ny), fields.dtype),
        scratch_shapes=[pltpu.SemaphoreType.DMA((4,))],
        compiler_params=pltpu.CompilerParams(vmem_limit_bytes=LIMIT),
        name="pack",
    )(plan, fields)


def choose_kernel(plan_ref, place_ref, pieces_ref, out_ref, sems):
    groups = pieces_ref.shape[0]
    block = place_ref[0] // (groups // 2)
    mover = plan_ref[block, 0]
    moved = plan_ref[2 + block, 0]
    pairs = []
    for g in range(groups):
        pairs += [
            (pieces_ref.at[mover, 0:8], out_ref.at[g, 0:8]),
            (pieces_ref.at[moved, 8:16], out_ref.at[g, 8:16]),
        ]
    run_copies(pairs, sems)


def choose(plan, place, pieces):
    return pl.pallas_call(
        choose_kernel,
        in_specs=[SMEM, SMEM, ANY],
        out_specs=ANY,
        out_shape=jax.ShapeDtypeStruct(pieces.shape, pieces.dtype),
        scratch_shapes=[pltpu.SemaphoreType.DMA((16,))],
        compiler_params=pltpu.CompilerParams(vmem_limit_bytes=LIMIT),
        name="choose",
    )(plan, place, pieces)


def kernel(*refs, rows, edges):
    metric_any, recv_any, test_any, *refs = refs
    if edges:
        low_any, high_any, acc_ref, out_ref, low_ref, high_ref, *refs = refs
    else:
        out_ref, *refs = refs
    metric_ref, recv_ref, test_ref, s_ref, wm_ref, phi_ref, f_ref, sems = refs
    groups, _, m, ny = recv_ref.shape
    n = groups * m
    f32 = jnp.float32
    count = len(rows)

    def flat(block):
        return block.astype(f32).reshape(n, ny)

    def row(c, r):
        if r < 0:
            return flat(low_ref[:, c])
        if r > 3:
            return flat(high_ref[:, c])
        return flat(recv_ref[:, 8 + 4 * c + r])

    @pl.when(pl.program_id(0) == 0)
    def _():
        pairs = [(metric_any, metric_ref), (recv_any, recv_ref), (test_any, test_ref)]
        if edges:
            pairs += [(low_any, low_ref), (high_any, high_ref)]
        run_copies(pairs, sems)
        lane = lax.broadcasted_iota(jnp.int32, (n, ny), 1)
        for c in range(2):
            for i, r in enumerate(rows):
                at = count * c + i
                mid = row(c, r)
                along_x = (row(c, r + 1) - row(c, r - 1)) * metric_ref[0, pl.ds(r, 1), :]
                after = jnp.where(lane == ny - 1, 0.0, pltpu.roll(mid, ny - 1, 1))
                before = jnp.where(lane == 0, 0.0, pltpu.roll(mid, 1, 1))
                along_y = (after - before) * metric_ref[1, pl.ds(r, 1), :]
                s_ref[0, at] = along_x.astype(jnp.bfloat16).astype(f32)
                s_ref[1, at] = along_y.astype(jnp.bfloat16).astype(f32)
                wm_ref[at] = flat(recv_ref[:, 4 * c + r]) * metric_ref[2, pl.ds(r, 1), :]
                phi_ref[:, pl.ds(at * ny, ny)] = test_ref[:, 4 * c + r].reshape(n, ny)

    base = pl.program_id(0) * JB
    for c in range(2):
        for i in range(count):
            at = count * c + i
            s0 = s_ref[0, at]
            s1 = s_ref[1, at]
            for b in range(JB):
                j = pl.ds(base + b, 1)
                field = wm_ref[i, j, :] * s0 + wm_ref[count + i, j, :] * s1
                f_ref[pl.ds(b * n, n), pl.ds(at * ny, ny)] = field.astype(jnp.bfloat16)
    res = lax.dot_general(f_ref[...], phi_ref[...], (((1,), (1,)), ((), ())), preferred_element_type=f32)
    res = res.reshape(JB, n, n)
    res = jnp.concatenate([res[:, : n // 2], res[:, n // 2 :]], axis=2)
    if edges:
        res = res + acc_ref[...]
    out_ref[...] = res.astype(out_ref.dtype)


def project(metric, recv, test, rows, edges=None):
    groups, _, m, ny = recv.shape
    n = groups * m
    width = 2 * len(rows)
    block = pl.BlockSpec((JB, n // 2, 2 * n), lambda i: (i, 0, 0))
    scratch = [
        pltpu.VMEM(metric.shape, metric.dtype),
        pltpu.VMEM(recv.shape, recv.dtype),
        pltpu.VMEM(test.shape, test.dtype),
        pltpu.VMEM((2, width, n, ny), jnp.float32),
        pltpu.VMEM((width, n, ny), jnp.float32),
        pltpu.VMEM((n, width * ny), jnp.bfloat16),
        pltpu.VMEM((JB * n, width * ny), jnp.bfloat16),
        pltpu.SemaphoreType.DMA((5,)),
    ]
    args = [metric, recv, test]
    specs = [ANY, ANY, ANY]
    if edges:
        args += edges
        specs += [ANY, ANY, block]
        scratch = [pltpu.VMEM(edges[0].shape, edges[0].dtype), pltpu.VMEM(edges[1].shape, edges[1].dtype)] + scratch
    return pl.pallas_call(
        lambda *refs: kernel(*refs, rows=rows, edges=bool(edges)),
        grid=(n // JB,),
        in_specs=specs,
        out_specs=block,
        out_shape=jax.ShapeDtypeStruct((n, n // 2, 2 * n), jnp.bfloat16 if edges else jnp.float32),
        scratch_shapes=scratch,
        compiler_params=pltpu.CompilerParams(dimension_semantics=("arbitrary",), vmem_limit_bytes=LIMIT),
        name="project_edges" if edges else "project_middle",
    )(*args)


def body(mode_fields, metric, plan):
    n = mode_fields.shape[0]
    ny = mode_fields.shape[3]
    groups = lax.axis_size(MODE)
    m = n // groups
    fields = mode_fields.reshape(groups, m, 2, 4, ny).transpose(0, 2, 3, 1, 4).reshape(groups, 8, m, ny)
    pieces = lax.all_to_all(pack(plan, fields), MODE, 0, 0, tiled=True)
    place = lax.axis_index(MODE).astype(jnp.int32).reshape(1)
    recv = lax.all_to_all(choose(plan, place, pieces), MODE, 0, 0, tiled=True)
    count = lax.axis_size(SPACE)
    forward = [(i, i + 1) for i in range(count - 1)]
    backward = [(i + 1, i) for i in range(count - 1)]
    carried = recv[:, 8:].reshape(groups, 2, 4, m, ny)
    low = lax.ppermute(carried[:, :, 3], SPACE, forward)
    high = lax.ppermute(carried[:, :, 0], SPACE, backward)
    middle = project(metric, recv, fields, (1, 2))
    shares = project(metric, recv, fields, (0, 3), [low, high, middle])
    shares = lax.all_to_all(shares, SPACE, 0, 0, tiled=True)
    norm_factor = float(4 * count * ny) ** (-0.5)
    total = jnp.sum(shares.astype(jnp.float32), axis=0) * norm_factor
    return jnp.concatenate([total[:, :n], total[:, n:]], axis=0)


def solution(mesh):
    fine = Mesh(mesh.devices.reshape(4, 2, 8, 4, 2), ("x", "zl", "y", "zh", "c"))
    return jax.shard_map(
        body,
        mesh=fine,
        in_specs=(P(MODE, None, SPACE, None), P(None, SPACE, None), P()),
        out_specs=P(SPACE, MODE),
        check_vma=False,
    )
```

```python
import jax
import jax.numpy as jnp
from jax import lax
from jax.experimental import pallas as pl
from jax.experimental.pallas import tpu as pltpu
from jax.sharding import Mesh, PartitionSpec as P

MODE = ("x", "zl")
SPACE = ("y", "zh", "c")
JB = 8
LIMIT = 16 * 2**20
SMEM = pl.BlockSpec(memory_space=pltpu.SMEM)
VMEM = pl.BlockSpec(memory_space=pltpu.VMEM)


def pack_kernel(plan_ref, place_ref, fields_ref, out_ref):
    del place_ref
    groups, _, m, ny = fields_ref.shape
    half = groups // 2
    for b in range(2):
        mover = plan_ref[1, b] * half
        moved = plan_ref[1, 2 + b] * half
        for g in range(half):
            out_ref[b * half + g, 0:8] = fields_ref[mover + g]
            out_ref[b * half + g, 8:16] = fields_ref[moved + g]


def pack(plan, place, fields):
    groups, _, m, ny = fields.shape
    return pl.pallas_call(
        pack_kernel,
        in_specs=[SMEM, SMEM, VMEM],
        out_specs=VMEM,
        out_shape=jax.ShapeDtypeStruct((groups, 16, m, ny), fields.dtype),
        compiler_params=pltpu.CompilerParams(vmem_limit_bytes=LIMIT),
        name="pack",
    )(plan, place, fields)


def choose_kernel(plan_ref, place_ref, pieces_ref, out_ref):
    groups = pieces_ref.shape[0]
    block = place_ref[0] // (groups // 2)
    mover = pieces_ref[plan_ref[0, block], 0:8]
    moved = pieces_ref[plan_ref[0, 2 + block], 8:16]
    for g in range(groups):
        out_ref[g, 0:8] = mover
        out_ref[g, 8:16] = moved


def choose(plan, place, pieces):
    return pl.pallas_call(
        choose_kernel,
        in_specs=[SMEM, SMEM, VMEM],
        out_specs=VMEM,
        out_shape=jax.ShapeDtypeStruct(pieces.shape, pieces.dtype),
        compiler_params=pltpu.CompilerParams(vmem_limit_bytes=LIMIT),
        name="choose",
    )(plan, place, pieces)


def kernel(*refs, rows, edges):
    metric_ref, recv_ref, test_ref, *refs = refs
    if edges:
        low_ref, high_ref, acc_ref, *refs = refs
    out_ref, s_ref, wm_ref, phi_ref, f_ref = refs
    groups, _, m, ny = recv_ref.shape
    n = groups * m
    f32 = jnp.float32
    count = len(rows)

    def flat(block):
        return block.astype(f32).reshape(n, ny)

    def row(c, r):
        if r < 0:
            return flat(low_ref[:, c])
        if r > 3:
            return flat(high_ref[:, c])
        return flat(recv_ref[:, 8 + 4 * c + r])

    @pl.when(pl.program_id(0) == 0)
    def _():
        lane = lax.broadcasted_iota(jnp.int32, (n, ny), 1)
        for c in range(2):
            for i, r in enumerate(rows):
                at = count * c + i
                mid = row(c, r)
                along_x = (row(c, r + 1) - row(c, r - 1)) * metric_ref[0, pl.ds(r, 1), :]
                after = jnp.where(lane == ny - 1, 0.0, pltpu.roll(mid, ny - 1, 1))
                before = jnp.where(lane == 0, 0.0, pltpu.roll(mid, 1, 1))
                along_y = (after - before) * metric_ref[1, pl.ds(r, 1), :]
                s_ref[0, at] = along_x.astype(jnp.bfloat16).astype(f32)
                s_ref[1, at] = along_y.astype(jnp.bfloat16).astype(f32)
                wm_ref[at] = flat(recv_ref[:, 4 * c + r]) * metric_ref[2, pl.ds(r, 1), :]
                phi_ref[:, pl.ds(at * ny, ny)] = test_ref[:, 4 * c + r].reshape(n, ny)

    base = pl.program_id(0) * JB
    for c in range(2):
        for i in range(count):
            at = count * c + i
            s0 = s_ref[0, at]
            s1 = s_ref[1, at]
            for b in range(JB):
                j = pl.ds(base + b, 1)
                field = wm_ref[i, j, :] * s0 + wm_ref[count + i, j, :] * s1
                f_ref[pl.ds(b * n, n), pl.ds(at * ny, ny)] = field.astype(jnp.bfloat16)
    res = lax.dot_general(f_ref[...], phi_ref[...], (((1,), (1,)), ((), ())), preferred_element_type=f32)
    res = res.reshape(JB, n, n)
    res = jnp.concatenate([res[:, : n // 2], res[:, n // 2 :]], axis=2)
    here = pl.ds(base, JB)
    if edges:
        res = res + acc_ref[here]
    out_ref[here] = res.astype(out_ref.dtype)


def project(metric, recv, test, rows, edges=None):
    groups, _, m, ny = recv.shape
    n = groups * m
    width = 2 * len(rows)
    args = [metric, recv, test] + (edges or [])
    return pl.pallas_call(
        lambda *refs: kernel(*refs, rows=rows, edges=bool(edges)),
        grid=(n // JB,),
        in_specs=[VMEM] * len(args),
        out_specs=VMEM,
        out_shape=jax.ShapeDtypeStruct((n, n // 2, 2 * n), jnp.bfloat16 if edges else jnp.float32),
        scratch_shapes=[
            pltpu.VMEM((2, width, n, ny), jnp.float32),
            pltpu.VMEM((width, n, ny), jnp.float32),
            pltpu.VMEM((n, width * ny), jnp.bfloat16),
            pltpu.VMEM((JB * n, width * ny), jnp.bfloat16),
        ],
        compiler_params=pltpu.CompilerParams(dimension_semantics=("arbitrary",), vmem_limit_bytes=LIMIT),
        name="project_edges" if edges else "project_middle",
    )(*args)


def body(mode_fields, metric, plan):
    n = mode_fields.shape[0]
    ny = mode_fields.shape[3]
    groups = lax.axis_size(MODE)
    m = n // groups
    fields = mode_fields.reshape(groups, m, 2, 4, ny).transpose(0, 2, 3, 1, 4).reshape(groups, 8, m, ny)
    place = lax.axis_index(MODE).astype(jnp.int32).reshape(1)
    pieces = lax.all_to_all(pack(plan.T, place, fields), MODE, 0, 0, tiled=True)
    recv = lax.all_to_all(choose(plan.T, place, pieces), MODE, 0, 0, tiled=True)
    count = lax.axis_size(SPACE)
    forward = [(i, i + 1) for i in range(count - 1)]
    backward = [(i + 1, i) for i in range(count - 1)]
    carried = recv[:, 8:].reshape(groups, 2, 4, m, ny)
    low = lax.ppermute(carried[:, :, 3], SPACE, forward)
    high = lax.ppermute(carried[:, :, 0], SPACE, backward)
    middle = project(metric, recv, fields, (1, 2))
    shares = project(metric, recv, fields, (0, 3), [low, high, middle])
    shares = lax.all_to_all(shares, SPACE, 0, 0, tiled=True)
    norm_factor = float(4 * count * ny) ** (-0.5)
    total = jnp.sum(shares.astype(jnp.float32), axis=0) * norm_factor
    return jnp.concatenate([total[:, :n], total[:, n:]], axis=0)


def solution(mesh):
    fine = Mesh(mesh.devices.reshape(4, 2, 8, 4, 2), ("x", "zl", "y", "zh", "c"))
    return jax.shard_map(
        body,
        mesh=fine,
        in_specs=(P(MODE, None, SPACE, None), P(None, SPACE, None), P()),
        out_specs=P(SPACE, MODE),
        check_vma=False,
    )
```

```python
import jax
import jax.numpy as jnp
from jax import lax
from jax.experimental import pallas as pl
from jax.experimental.pallas import tpu as pltpu
from jax.sharding import Mesh, PartitionSpec as P

MODE = ("x", "zl")
SPACE = ("y", "zh", "c")
JB = 8
LIMIT = 16 * 2**20
SMEM = pl.BlockSpec(memory_space=pltpu.SMEM)
VMEM = pl.BlockSpec(memory_space=pltpu.VMEM)


def pack_kernel(plan_ref, place_ref, fields_ref, out_ref):
    del place_ref
    groups, _, m, ny = fields_ref.shape
    half = groups // 2
    for b in range(2):
        mover = plan_ref[1, b] * half
        moved = plan_ref[1, 2 + b] * half
        for g in range(half):
            out_ref[b * half + g, 0:8] = fields_ref[mover + g]
            out_ref[b * half + g, 8:16] = fields_ref[moved + g]


def pack(plan, place, fields):
    groups, _, m, ny = fields.shape
    return pl.pallas_call(
        pack_kernel,
        in_specs=[SMEM, SMEM, VMEM],
        out_specs=VMEM,
        out_shape=jax.ShapeDtypeStruct((groups, 16, m, ny), fields.dtype),
        compiler_params=pltpu.CompilerParams(vmem_limit_bytes=LIMIT),
        name="pack",
    )(plan, place, fields)


def choose_kernel(plan_ref, place_ref, pieces_ref, out_ref):
    groups = pieces_ref.shape[0]
    block = place_ref[0] // groups
    mover = pieces_ref[plan_ref[0, block], 0:8]
    moved = pieces_ref[plan_ref[0, 2 + block], 8:16]
    for g in range(groups):
        out_ref[g, 0:8] = mover
        out_ref[g, 8:16] = moved


def choose(plan, place, pieces):
    return pl.pallas_call(
        choose_kernel,
        in_specs=[SMEM, SMEM, VMEM],
        out_specs=VMEM,
        out_shape=jax.ShapeDtypeStruct(pieces.shape, pieces.dtype),
        compiler_params=pltpu.CompilerParams(vmem_limit_bytes=LIMIT),
        name="choose",
    )(plan, place, pieces)


def edge_kernel(place_ref, recv_ref, inner_ref, outer_ref):
    core = place_ref[0] % 2
    for c in range(2):
        inner_ref[:, c] = recv_ref[:, 8 + 4 * c + 3 * (1 - core)]
        outer_ref[:, c] = recv_ref[:, 8 + 4 * c + 3 * core]


def edge_rows(place, recv):
    groups, _, m, ny = recv.shape
    shape = jax.ShapeDtypeStruct((groups, 2, m, ny), recv.dtype)
    return pl.pallas_call(
        edge_kernel,
        in_specs=[SMEM, VMEM],
        out_specs=[VMEM, VMEM],
        out_shape=[shape, shape],
        compiler_params=pltpu.CompilerParams(vmem_limit_bytes=LIMIT),
        name="edge_rows",
    )(place, recv)


def kernel(*refs, rows, edges):
    metric_ref, recv_ref, test_ref, *refs = refs
    if edges:
        place_ref, inner_ref, outer_ref, acc_ref, *refs = refs
        first = place_ref[0] % 2 == 0
    out_ref, s_ref, wm_ref, phi_ref, even_ref, odd_ref = refs
    groups, _, m, ny = recv_ref.shape
    n = groups * m
    f32 = jnp.float32
    count = len(rows)

    def flat(block):
        return block.astype(f32).reshape(n, ny)

    def row(c, r):
        if r < 0:
            return jnp.where(first, flat(outer_ref[:, c]), flat(inner_ref[:, c]))
        if r > 3:
            return jnp.where(first, flat(inner_ref[:, c]), flat(outer_ref[:, c]))
        return flat(recv_ref[:, 8 + 4 * c + r])

    lane = lax.broadcasted_iota(jnp.int32, (n, ny), 1)
    for c in range(2):
        for i, r in enumerate(rows):
            at = count * c + i
            mid = row(c, r)
            along_x = (row(c, r + 1) - row(c, r - 1)) * metric_ref[0, pl.ds(r, 1), :]
            after = jnp.where(lane == ny - 1, 0.0, pltpu.roll(mid, ny - 1, 1))
            before = jnp.where(lane == 0, 0.0, pltpu.roll(mid, 1, 1))
            along_y = (after - before) * metric_ref[1, pl.ds(r, 1), :]
            s_ref[0, at] = along_x.astype(jnp.bfloat16).astype(f32)
            s_ref[1, at] = along_y.astype(jnp.bfloat16).astype(f32)
            wm_ref[at] = flat(recv_ref[:, 4 * c + r]) * metric_ref[2, pl.ds(r, 1), :]
            phi_ref[:, pl.ds(at * ny, ny)] = test_ref[:, 4 * c + r].reshape(n, ny)

    def build(block, f_ref):
        for at in range(2 * count):
            i = at % count
            s0 = s_ref[0, at]
            s1 = s_ref[1, at]
            for b in range(JB):
                j = pl.ds(block * JB + b, 1)
                field = wm_ref[i, j, :] * s0 + wm_ref[count + i, j, :] * s1
                f_ref[pl.ds(b * n, n), pl.ds(at * ny, ny)] = field.astype(jnp.bfloat16)

    def multiply(block, f_ref):
        res = lax.dot_general(f_ref[...], phi_ref[...], (((1,), (1,)), ((), ())), preferred_element_type=f32)
        res = res.reshape(JB, n, n)
        res = jnp.concatenate([res[:, : n // 2], res[:, n // 2 :]], axis=2)
        here = pl.ds(block * JB, JB)
        if edges:
            res = res + acc_ref[here]
        out_ref[here] = res.astype(out_ref.dtype)

    blocks = n // JB
    buffers = (even_ref, odd_ref)
    build(0, even_ref)
    for block in range(blocks):
        if block + 1 < blocks:
            build(block + 1, buffers[(block + 1) % 2])
        multiply(block, buffers[block % 2])


def project(metric, recv, test, rows, edges=None):
    groups, _, m, ny = recv.shape
    n = groups * m
    width = 2 * len(rows)
    args = [metric, recv, test] + (edges or [])
    return pl.pallas_call(
        lambda *refs: kernel(*refs, rows=rows, edges=bool(edges)),
        in_specs=[VMEM] * 3 + ([SMEM] + [VMEM] * 3 if edges else []),
        out_specs=VMEM,
        out_shape=jax.ShapeDtypeStruct((n, n // 2, 2 * n), jnp.bfloat16 if edges else jnp.float32),
        scratch_shapes=[
            pltpu.VMEM((2, width, n, ny), jnp.float32),
            pltpu.VMEM((width, n, ny), jnp.float32),
            pltpu.VMEM((n, width * ny), jnp.bfloat16),
            pltpu.VMEM((JB * n, width * ny), jnp.bfloat16),
            pltpu.VMEM((JB * n, width * ny), jnp.bfloat16),
        ],
        compiler_params=pltpu.CompilerParams(vmem_limit_bytes=LIMIT),
        name="project_edges" if edges else "project_middle",
    )(*args)


def body(mode_fields, metric, plan):
    n = mode_fields.shape[0]
    ny = mode_fields.shape[3]
    groups = lax.axis_size(MODE)
    m = n // groups
    fields = mode_fields.reshape(groups, m, 2, 4, ny).transpose(0, 2, 3, 1, 4).reshape(groups, 8, m, ny)
    place = lax.axis_index(MODE + ("c",)).astype(jnp.int32).reshape(1)
    pieces = lax.all_to_all(pack(plan.T, place, fields), MODE, 0, 0, tiled=True)
    recv = lax.all_to_all(choose(plan.T, place, pieces), MODE, 0, 0, tiled=True)
    count = lax.axis_size(SPACE)
    inner, outer = edge_rows(place, recv)
    between = [(i, i + 1 if i % 2 else i - 1) for i in range(1, count - 1)]
    outer = lax.ppermute(outer, SPACE, between)
    inner = lax.ppermute(inner, "c", [(0, 1), (1, 0)])
    middle = project(metric, recv, fields, (1, 2))
    shares = project(metric, recv, fields, (0, 3), [place, inner, outer, middle])
    shares = lax.all_to_all(shares, SPACE, 0, 0, tiled=True)
    norm_factor = float(4 * count * ny) ** (-0.5)
    total = jnp.sum(shares.astype(jnp.float32), axis=0) * norm_factor
    return jnp.concatenate([total[:, :n], total[:, n:]], axis=0)


def solution(mesh):
    fine = Mesh(mesh.devices.reshape(4, 2, 8, 4, 2), ("x", "zl", "y", "zh", "c"))
    return jax.shard_map(
        body,
        mesh=fine,
        in_specs=(P(MODE, None, SPACE, None), P(None, SPACE, None), P()),
        out_specs=P(SPACE, MODE),
        check_vma=False,
    )
```

```python
import jax
import jax.numpy as jnp
from jax import lax
from jax.experimental import pallas as pl
from jax.experimental.pallas import tpu as pltpu
from jax.sharding import Mesh, PartitionSpec as P


MODE = ("x", "zl")
SPACE = ("y", "zh", "c")
JB = 8
LIMIT = 16 * 2**20
SMEM = pl.BlockSpec(memory_space=pltpu.SMEM)
VMEM = pl.BlockSpec(memory_space=pltpu.VMEM)


def pack_kernel(plan_ref, place_ref, fields_ref, out_ref):
    del place_ref
    groups, _, _, _ = fields_ref.shape
    half = groups // 2
    for b in range(2):
        mover = plan_ref[1, b] * half
        moved = plan_ref[1, 2 + b] * half
        for g in range(half):
            out_ref[b * half + g, 0:8] = fields_ref[mover + g]
            out_ref[b * half + g, 8:16] = fields_ref[moved + g]


def pack(plan, place, fields):
    groups, _, m, ny = fields.shape
    return pl.pallas_call(
        pack_kernel,
        in_specs=[SMEM, SMEM, VMEM],
        out_specs=VMEM,
        out_shape=jax.ShapeDtypeStruct((groups, 16, m, ny), fields.dtype),
        compiler_params=pltpu.CompilerParams(vmem_limit_bytes=LIMIT),
        name="pack",
    )(plan, place, fields)


def choose_kernel(plan_ref, place_ref, pieces_ref, out_ref):
    groups = pieces_ref.shape[0]
    block = place_ref[0] // groups
    mover = pieces_ref[plan_ref[0, block], 0:8]
    moved = pieces_ref[plan_ref[0, 2 + block], 8:16]
    for g in range(groups):
        out_ref[g, 0:8] = mover
        out_ref[g, 8:16] = moved


def choose(plan, place, pieces):
    return pl.pallas_call(
        choose_kernel,
        in_specs=[SMEM, SMEM, VMEM],
        out_specs=VMEM,
        out_shape=jax.ShapeDtypeStruct(pieces.shape, pieces.dtype),
        compiler_params=pltpu.CompilerParams(vmem_limit_bytes=LIMIT),
        name="choose",
    )(plan, place, pieces)


def edge_kernel(place_ref, recv_ref, inner_ref, outer_ref):
    core = place_ref[0] % 2
    for c in range(2):
        inner_ref[:, c] = recv_ref[:, 8 + 4 * c + 3 * (1 - core)]
        outer_ref[:, c] = recv_ref[:, 8 + 4 * c + 3 * core]


def edge_rows(place, recv):
    groups, _, m, ny = recv.shape
    shape = jax.ShapeDtypeStruct((groups, 2, m, ny), recv.dtype)
    return pl.pallas_call(
        edge_kernel,
        in_specs=[SMEM, VMEM],
        out_specs=[VMEM, VMEM],
        out_shape=[shape, shape],
        compiler_params=pltpu.CompilerParams(vmem_limit_bytes=LIMIT),
        name="edge_rows",
    )(place, recv)


def kernel(*refs, rows, edges, send):
    metric_ref, recv_ref, test_ref, *refs = refs
    if edges:
        place_ref, inner_ref, outer_ref, acc_ref, *refs = refs
        core = place_ref[0] % 2
        first = core == 0
    out_ref, s_ref, wm_ref, phi_ref, even_ref, odd_ref = refs
    groups, _, m, ny = recv_ref.shape
    n = groups * m
    f32 = jnp.float32
    count = len(rows)

    def flat(block):
        return block.astype(f32).reshape(n, ny)

    def row(c, r):
        if r < 0:
            return jnp.where(first, flat(outer_ref[:, c]), flat(inner_ref[:, c]))
        if r > 3:
            return jnp.where(first, flat(inner_ref[:, c]), flat(outer_ref[:, c]))
        return flat(recv_ref[:, 8 + 4 * c + r])

    lane = lax.broadcasted_iota(jnp.int32, (n, ny), 1)
    for c in range(2):
        for i, r in enumerate(rows):
            at = count * c + i
            mid = row(c, r)
            along_x = (row(c, r + 1) - row(c, r - 1)) * metric_ref[0, pl.ds(r, 1), :]
            after = jnp.where(lane == ny - 1, 0.0, pltpu.roll(mid, ny - 1, 1))
            before = jnp.where(lane == 0, 0.0, pltpu.roll(mid, 1, 1))
            along_y = (after - before) * metric_ref[1, pl.ds(r, 1), :]
            s_ref[0, at] = along_x.astype(jnp.bfloat16).astype(f32)
            s_ref[1, at] = along_y.astype(jnp.bfloat16).astype(f32)
            wm_ref[at] = flat(recv_ref[:, 4 * c + r]) * metric_ref[2, pl.ds(r, 1), :]
            phi_ref[:, pl.ds(at * ny, ny)] = test_ref[:, 4 * c + r].reshape(n, ny)

    pairs = n // 2
    if edges:
        side = 1 - core if send else core

    def build(block, f_ref):
        for at in range(2 * count):
            i = at % count
            s0 = s_ref[0, at]
            s1 = s_ref[1, at]
            for b in range(JB):
                slot = block * JB + b
                j = pl.ds(2 * slot + side if edges else 2 * (slot % pairs) + slot // pairs, 1)
                field = wm_ref[i, j, :] * s0 + wm_ref[count + i, j, :] * s1
                f_ref[pl.ds(b * n, n), pl.ds(at * ny, ny)] = field.astype(jnp.bfloat16)

    def multiply(block, f_ref):
        res = lax.dot_general(f_ref[...], phi_ref[...], (((1,), (1,)), ((), ())), preferred_element_type=f32)
        res = res.reshape(JB, n, n)
        res = jnp.concatenate([res[:, : n // 2], res[:, n // 2 :]], axis=2)
        here = pl.ds(block * JB, JB)
        if edges:
            res = res + acc_ref[pl.ds(side * pairs + block * JB, JB)]
        out_ref[here] = res.astype(out_ref.dtype)

    blocks = out_ref.shape[0] // JB
    buffers = (even_ref, odd_ref)
    build(0, even_ref)
    for block in range(blocks):
        if block + 1 < blocks:
            build(block + 1, buffers[(block + 1) % 2])
        multiply(block, buffers[block % 2])


def project(metric, recv, test, rows, edges=None, send=False):
    groups, _, m, ny = recv.shape
    n = groups * m
    width = 2 * len(rows)
    args = [metric, recv, test] + (edges or [])
    return pl.pallas_call(
        lambda *refs: kernel(*refs, rows=rows, edges=bool(edges), send=send),
        in_specs=[VMEM] * 3 + ([SMEM] + [VMEM] * 3 if edges else []),
        out_specs=VMEM,
        out_shape=jax.ShapeDtypeStruct((n // 2 if edges else n, n // 2, 2 * n), jnp.float32),
        scratch_shapes=[
            pltpu.VMEM((2, width, n, ny), jnp.float32),
            pltpu.VMEM((width, n, ny), jnp.float32),
            pltpu.VMEM((n, width * ny), jnp.bfloat16),
            pltpu.VMEM((JB * n, width * ny), jnp.bfloat16),
            pltpu.VMEM((JB * n, width * ny), jnp.bfloat16),
        ],
        compiler_params=pltpu.CompilerParams(vmem_limit_bytes=LIMIT),
        name=("project_send" if send else "project_keep") if edges else "project_middle",
    )(*args)


def body(mode_fields, metric, plan):
    n = mode_fields.shape[0]
    ny = mode_fields.shape[3]
    groups = lax.axis_size(MODE)
    m = n // groups
    fields = mode_fields.reshape(groups, m, 2, 4, ny).transpose(0, 2, 3, 1, 4).reshape(groups, 8, m, ny)
    place = lax.axis_index(MODE + ("c",)).astype(jnp.int32).reshape(1)
    pieces = lax.all_to_all(pack(plan.T, place, fields), MODE, 0, 0, tiled=True)
    recv = lax.all_to_all(choose(plan.T, place, pieces), MODE, 0, 0, tiled=True)
    count = lax.axis_size(SPACE)
    inner, outer = edge_rows(place, recv)
    between = [(i, i + 1 if i % 2 else i - 1) for i in range(1, count - 1)]
    outer = lax.ppermute(outer, SPACE, between)
    inner = lax.ppermute(inner, "c", [(0, 1), (1, 0)])
    middle = project(metric, recv, fields, (1, 2))
    edges = [place, inner, outer, middle]
    sent = project(metric, recv, fields, (0, 3), edges, send=True)
    other = lax.ppermute(sent, "c", [(0, 1), (1, 0)])
    kept = project(metric, recv, fields, (0, 3), edges)
    shares = lax.all_to_all((kept + other).astype(jnp.bfloat16), ("y", "zh"), 0, 0, tiled=True)
    norm_factor = float(4 * count * ny) ** (-0.5)
    total = jnp.sum(shares.astype(jnp.float32), axis=0) * norm_factor
    return jnp.concatenate([total[:, :n], total[:, n:]], axis=0)


def solution(mesh):
    fine = Mesh(mesh.devices.reshape(4, 2, 8, 4, 2), ("x", "zl", "y", "zh", "c"))
    return jax.shard_map(
        body,
        mesh=fine,
        in_specs=(P(MODE, None, SPACE, None), P(None, SPACE, None), P()),
        out_specs=P(SPACE, MODE),
        check_vma=False,
    )
```

```python
import jax
import jax.numpy as jnp
from jax import lax
from jax.experimental import pallas as pl
from jax.experimental.pallas import tpu as pltpu
from jax.sharding import Mesh, PartitionSpec as P


MODE = ("x", "zl")
SPACE = ("y", "zh", "c")
JB = 8
LIMIT = 16 * 2**20
SMEM = pl.BlockSpec(memory_space=pltpu.SMEM)
HBM = pl.BlockSpec(memory_space=pltpu.HBM)
VMEM = pl.BlockSpec(memory_space=pltpu.VMEM)


def pack_kernel(plan_hbm, place_ref, raw_hbm, fields_ref, out_ref, pick_ref, plan_ref, raw_ref, sems):
    raw_copy = pltpu.make_async_copy(raw_hbm, raw_ref, sems.at[0])
    plan_copy = pltpu.make_async_copy(plan_hbm, plan_ref, sems.at[1])
    raw_copy.start()
    plan_copy.start()
    raw_copy.wait()
    groups, _, m, _ = fields_ref.shape
    for g in range(groups):
        for c in range(2):
            block = raw_ref[g * m : (g + 1) * m, c].astype(jnp.float32)
            fields_ref[g, 4 * c : 4 * c + 4] = jnp.swapaxes(block, 0, 1).astype(fields_ref.dtype)
    plan_copy.wait()
    half = groups // 2
    for b in range(2):
        mover = plan_ref[1, b] * half
        moved = plan_ref[1, 2 + b] * half
        for g in range(half):
            out_ref[b * half + g, 0:8] = fields_ref[mover + g]
            out_ref[b * half + g, 8:16] = fields_ref[moved + g]
    block = place_ref[0] // groups
    for kind in range(2):
        owner = plan_ref[0, 2 * kind + block]
        for g in range(groups):
            pick_ref[kind, g] = jnp.full(pick_ref.shape[2:], jnp.where(owner == g, 1.0, 0.0), pick_ref.dtype)


def pack(plan, place, mode_fields, groups):
    modes, _, _, ny = mode_fields.shape
    m = modes // groups
    return pl.pallas_call(
        pack_kernel,
        in_specs=[HBM, SMEM, HBM],
        out_specs=[VMEM, VMEM, VMEM],
        out_shape=[
            jax.ShapeDtypeStruct((groups, 8, m, ny), mode_fields.dtype),
            jax.ShapeDtypeStruct((groups, 16, m, ny), mode_fields.dtype),
            jax.ShapeDtypeStruct((2, groups, m, ny), jnp.float32),
        ],
        scratch_shapes=[
            pltpu.SMEM(plan.shape, plan.dtype),
            pltpu.VMEM(mode_fields.shape, mode_fields.dtype),
            pltpu.SemaphoreType.DMA((2,)),
        ],
        compiler_params=pltpu.CompilerParams(vmem_limit_bytes=LIMIT),
        name="pack",
    )(plan, place, mode_fields)


def choose_kernel(pick_ref, pieces_ref, out_ref):
    groups = pieces_ref.shape[0]
    for r in range(16):
        piece = sum(pieces_ref[g, r].astype(jnp.float32) * pick_ref[r // 8, g] for g in range(groups))
        for g in range(groups):
            out_ref[g, r] = piece.astype(out_ref.dtype)


def choose(pick, pieces):
    return pl.pallas_call(
        choose_kernel,
        in_specs=[VMEM, VMEM],
        out_specs=VMEM,
        out_shape=jax.ShapeDtypeStruct(pieces.shape, pieces.dtype),
        compiler_params=pltpu.CompilerParams(vmem_limit_bytes=LIMIT),
        name="choose",
    )(pick, pieces)


def edge_kernel(place_ref, recv_ref, inner_ref, outer_ref):
    core = place_ref[0] % 2
    for c in range(2):
        inner_ref[:, c] = recv_ref[:, 8 + 4 * c + 3 * (1 - core)]
        outer_ref[:, c] = recv_ref[:, 8 + 4 * c + 3 * core]


def edge_rows(place, recv):
    groups, _, m, ny = recv.shape
    shape = jax.ShapeDtypeStruct((groups, 2, m, ny), recv.dtype)
    return pl.pallas_call(
        edge_kernel,
        in_specs=[SMEM, VMEM],
        out_specs=[VMEM, VMEM],
        out_shape=[shape, shape],
        compiler_params=pltpu.CompilerParams(vmem_limit_bytes=LIMIT),
        name="edge_rows",
    )(place, recv)


def kernel(*refs, rows, edges, send):
    metric_ref, recv_ref, test_ref, *refs = refs
    if edges:
        place_ref, inner_ref, outer_ref, acc_ref, *refs = refs
        core = place_ref[0] % 2
        first = core == 0
    out_ref, s_ref, wm_ref, phi_ref, even_ref, odd_ref = refs
    groups, _, m, ny = recv_ref.shape
    n = groups * m
    f32 = jnp.float32
    count = len(rows)

    def flat(block):
        return block.astype(f32).reshape(n, ny)

    def row(c, r):
        if r < 0:
            return jnp.where(first, flat(outer_ref[:, c]), flat(inner_ref[:, c]))
        if r > 3:
            return jnp.where(first, flat(inner_ref[:, c]), flat(outer_ref[:, c]))
        return flat(recv_ref[:, 8 + 4 * c + r])

    lane = lax.broadcasted_iota(jnp.int32, (n, ny), 1)
    for c in range(2):
        for i, r in enumerate(rows):
            at = count * c + i
            mid = row(c, r)
            along_x = (row(c, r + 1) - row(c, r - 1)) * metric_ref[0, pl.ds(r, 1), :]
            after = jnp.where(lane == ny - 1, 0.0, pltpu.roll(mid, ny - 1, 1))
            before = jnp.where(lane == 0, 0.0, pltpu.roll(mid, 1, 1))
            along_y = (after - before) * metric_ref[1, pl.ds(r, 1), :]
            s_ref[0, at] = along_x.astype(jnp.bfloat16).astype(f32)
            s_ref[1, at] = along_y.astype(jnp.bfloat16).astype(f32)
            wm_ref[at] = flat(recv_ref[:, 4 * c + r]) * metric_ref[2, pl.ds(r, 1), :]
            phi_ref[:, pl.ds(at * ny, ny)] = test_ref[:, 4 * c + r].reshape(n, ny)

    pairs = n // 2
    if edges:
        side = 1 - core if send else core

    def build(block, f_ref):
        for at in range(2 * count):
            i = at % count
            s0 = s_ref[0, at]
            s1 = s_ref[1, at]
            for b in range(JB):
                slot = block * JB + b
                j = pl.ds(2 * slot + side if edges else 2 * (slot % pairs) + slot // pairs, 1)
                field = wm_ref[i, j, :] * s0 + wm_ref[count + i, j, :] * s1
                f_ref[pl.ds(b * n, n), pl.ds(at * ny, ny)] = field.astype(jnp.bfloat16)

    def multiply(block, f_ref):
        res = lax.dot_general(f_ref[...], phi_ref[...], (((1,), (1,)), ((), ())), preferred_element_type=f32)
        res = res.reshape(JB, n, n)
        res = jnp.concatenate([res[:, : n // 2], res[:, n // 2 :]], axis=2)
        here = pl.ds(block * JB, JB)
        if edges:
            res = res + acc_ref[pl.ds(side * pairs + block * JB, JB)]
        out_ref[here] = res.astype(out_ref.dtype)

    blocks = out_ref.shape[0] // JB
    buffers = (even_ref, odd_ref)
    build(0, even_ref)
    for block in range(blocks):
        if block + 1 < blocks:
            build(block + 1, buffers[(block + 1) % 2])
        multiply(block, buffers[block % 2])


def project(metric, recv, test, rows, edges=None, send=False):
    groups, _, m, ny = recv.shape
    n = groups * m
    width = 2 * len(rows)
    args = [metric, recv, test] + (edges or [])
    return pl.pallas_call(
        lambda *refs: kernel(*refs, rows=rows, edges=bool(edges), send=send),
        in_specs=[VMEM] * 3 + ([SMEM] + [VMEM] * 3 if edges else []),
        out_specs=VMEM,
        out_shape=jax.ShapeDtypeStruct((n // 2 if edges else n, n // 2, 2 * n), jnp.float32),
        scratch_shapes=[
            pltpu.VMEM((2, width, n, ny), jnp.float32),
            pltpu.VMEM((width, n, ny), jnp.float32),
            pltpu.VMEM((n, width * ny), jnp.bfloat16),
            pltpu.VMEM((JB * n, width * ny), jnp.bfloat16),
            pltpu.VMEM((JB * n, width * ny), jnp.bfloat16),
        ],
        compiler_params=pltpu.CompilerParams(vmem_limit_bytes=LIMIT),
        name=("project_send" if send else "project_keep") if edges else "project_middle",
    )(*args)


def body(mode_fields, metric, plan):
    n = mode_fields.shape[0]
    ny = mode_fields.shape[3]
    groups = lax.axis_size(MODE)
    place = lax.axis_index(MODE + ("c",)).astype(jnp.int32).reshape(1)
    plan = pltpu.with_memory_space_constraint(plan.T, pltpu.HBM)
    raw = pltpu.with_memory_space_constraint(mode_fields, pltpu.HBM)
    fields, packed, pick = pack(plan, place, raw, groups)
    pieces = lax.all_to_all(packed, MODE, 0, 0, tiled=True)
    recv = lax.all_to_all(choose(pick, pieces), MODE, 0, 0, tiled=True)
    count = lax.axis_size(SPACE)
    inner, outer = edge_rows(place, recv)
    between = [(i, i + 1 if i % 2 else i - 1) for i in range(1, count - 1)]
    outer = lax.ppermute(outer, SPACE, between)
    inner = lax.ppermute(inner, "c", [(0, 1), (1, 0)])
    middle = project(metric, recv, fields, (1, 2))
    edges = [place, inner, outer, middle]
    sent = project(metric, recv, fields, (0, 3), edges, send=True)
    other = lax.ppermute(sent, "c", [(0, 1), (1, 0)])
    kept = project(metric, recv, fields, (0, 3), edges)
    shares = lax.all_to_all((kept + other).astype(jnp.bfloat16), ("y", "zh"), 0, 0, tiled=True)
    norm_factor = float(4 * count * ny) ** (-0.5)
    total = jnp.sum(shares.astype(jnp.float32), axis=0) * norm_factor
    return jnp.concatenate([total[:, :n], total[:, n:]], axis=0)


def solution(mesh):
    fine = Mesh(mesh.devices.reshape(4, 2, 8, 4, 2), ("x", "zl", "y", "zh", "c"))
    return jax.shard_map(
        body,
        mesh=fine,
        in_specs=(P(MODE, None, SPACE, None), P(None, SPACE, None), P()),
        out_specs=P(SPACE, MODE),
        check_vma=False,
    )
```

```python
import jax
import jax.numpy as jnp
from jax import lax
from jax.experimental import pallas as pl
from jax.experimental.pallas import tpu as pltpu
from jax.sharding import Mesh, PartitionSpec as P


MODE = ("x", "zl")
SPACE = ("y", "zh", "c")
JB = 4
LIMIT = 16 * 2**20
SMEM = pl.BlockSpec(memory_space=pltpu.SMEM)
HBM = pl.BlockSpec(memory_space=pltpu.HBM)
VMEM = pl.BlockSpec(memory_space=pltpu.VMEM)


def pack_kernel(plan_hbm, place_ref, raw_hbm, fields_ref, out_ref, pick_ref, plan_ref, raw_ref, sems):
    raw_copy = pltpu.make_async_copy(raw_hbm, raw_ref, sems.at[0])
    plan_copy = pltpu.make_async_copy(plan_hbm, plan_ref, sems.at[1])
    raw_copy.start()
    plan_copy.start()
    raw_copy.wait()
    groups, _, m, _ = fields_ref.shape
    for g in range(groups):
        for c in range(2):
            block = raw_ref[g * m : (g + 1) * m, c].astype(jnp.float32)
            fields_ref[g, 4 * c : 4 * c + 4] = jnp.swapaxes(block, 0, 1).astype(fields_ref.dtype)
    plan_copy.wait()
    half = groups // 2
    for b in range(2):
        mover = plan_ref[1, b] * half
        moved = plan_ref[1, 2 + b] * half
        for g in range(half):
            out_ref[b * half + g, 0:8] = fields_ref[mover + g]
            out_ref[b * half + g, 8:16] = fields_ref[moved + g]
    block = place_ref[0] // groups
    for kind in range(2):
        owner = plan_ref[0, 2 * kind + block]
        for g in range(groups):
            pick_ref[kind, g] = jnp.full(pick_ref.shape[2:], jnp.where(owner == g, 1.0, 0.0), pick_ref.dtype)


def pack(plan, place, mode_fields, groups):
    modes, _, _, ny = mode_fields.shape
    m = modes // groups
    return pl.pallas_call(
        pack_kernel,
        in_specs=[HBM, SMEM, HBM],
        out_specs=[VMEM, VMEM, VMEM],
        out_shape=[
            jax.ShapeDtypeStruct((groups, 8, m, ny), mode_fields.dtype),
            jax.ShapeDtypeStruct((groups, 16, m, ny), mode_fields.dtype),
            jax.ShapeDtypeStruct((2, groups, m, ny), jnp.float32),
        ],
        scratch_shapes=[
            pltpu.SMEM(plan.shape, plan.dtype),
            pltpu.VMEM(mode_fields.shape, mode_fields.dtype),
            pltpu.SemaphoreType.DMA((2,)),
        ],
        compiler_params=pltpu.CompilerParams(vmem_limit_bytes=LIMIT),
        name="pack",
    )(plan, place, mode_fields)


def choose_kernel(pick_ref, pieces_ref, out_ref):
    groups = pieces_ref.shape[0]
    for r in range(16):
        piece = sum(pieces_ref[g, r].astype(jnp.float32) * pick_ref[r // 8, g] for g in range(groups))
        for g in range(groups):
            out_ref[g, r] = piece.astype(out_ref.dtype)


def choose(pick, pieces):
    return pl.pallas_call(
        choose_kernel,
        in_specs=[VMEM, VMEM],
        out_specs=VMEM,
        out_shape=jax.ShapeDtypeStruct(pieces.shape, pieces.dtype),
        compiler_params=pltpu.CompilerParams(vmem_limit_bytes=LIMIT),
        name="choose",
    )(pick, pieces)


def edge_kernel(place_ref, recv_ref, inner_ref, outer_ref):
    core = place_ref[0] % 2
    for c in range(2):
        inner_ref[:, c] = recv_ref[:, 8 + 4 * c + 3 * (1 - core)]
        outer_ref[:, c] = recv_ref[:, 8 + 4 * c + 3 * core]


def edge_rows(place, recv):
    groups, _, m, ny = recv.shape
    shape = jax.ShapeDtypeStruct((groups, 2, m, ny), recv.dtype)
    return pl.pallas_call(
        edge_kernel,
        in_specs=[SMEM, VMEM],
        out_specs=[VMEM, VMEM],
        out_shape=[shape, shape],
        compiler_params=pltpu.CompilerParams(vmem_limit_bytes=LIMIT),
        name="edge_rows",
    )(place, recv)


def kernel(*refs, rows, edges, more, send):
    metric_ref, recv_ref, test_ref, place_ref, *refs = refs
    core = place_ref[0] % 2
    if edges:
        first = core == 0
        inner_ref, outer_ref, *refs = refs
    if more:
        acc_ref, *refs = refs
    out_ref, s_ref, wm_ref, phi_ref, even_ref, odd_ref = refs
    groups, _, m, ny = recv_ref.shape
    n = groups * m
    f32 = jnp.float32
    count = len(rows)

    def flat(block):
        return block.astype(f32).reshape(n, ny)

    def row(c, r):
        if r < 0:
            return jnp.where(first, flat(outer_ref[:, c]), flat(inner_ref[:, c]))
        if r > 3:
            return jnp.where(first, flat(inner_ref[:, c]), flat(outer_ref[:, c]))
        return flat(recv_ref[:, 8 + 4 * c + r])

    lane = lax.broadcasted_iota(jnp.int32, (n, ny), 1)
    for c in range(2):
        for i, r in enumerate(rows):
            at = count * c + i
            mid = row(c, r)
            along_x = (row(c, r + 1) - row(c, r - 1)) * metric_ref[0, pl.ds(r, 1), :]
            after = jnp.where(lane == ny - 1, 0.0, pltpu.roll(mid, ny - 1, 1))
            before = jnp.where(lane == 0, 0.0, pltpu.roll(mid, 1, 1))
            along_y = (after - before) * metric_ref[1, pl.ds(r, 1), :]
            s_ref[0, at] = along_x.astype(jnp.bfloat16).astype(f32)
            s_ref[1, at] = along_y.astype(jnp.bfloat16).astype(f32)
            wm_ref[at] = flat(recv_ref[:, 4 * c + r]) * metric_ref[2, pl.ds(r, 1), :]
            phi_ref[:, pl.ds(at * ny, ny)] = test_ref[:, 4 * c + r].reshape(n, ny)

    side = 1 - core if send else core

    def build(block, f_ref):
        for at in range(2 * count):
            i = at % count
            s0 = s_ref[0, at]
            s1 = s_ref[1, at]
            for b in range(JB):
                slot = block * JB + b
                j = pl.ds(2 * slot + side, 1)
                field = wm_ref[i, j, :] * s0 + wm_ref[count + i, j, :] * s1
                f_ref[pl.ds(b * n, n), pl.ds(at * ny, ny)] = field.astype(jnp.bfloat16)

    def multiply(block, f_ref):
        res = lax.dot_general(f_ref[...], phi_ref[...], (((1,), (1,)), ((), ())), preferred_element_type=f32)
        res = res.reshape(JB, n, n)
        res = jnp.concatenate([res[:, : n // 2], res[:, n // 2 :]], axis=2)
        here = pl.ds(block * JB, JB)
        if more:
            res = res + acc_ref[here]
        out_ref[here] = res.astype(out_ref.dtype)

    blocks = out_ref.shape[0] // JB
    buffers = (even_ref, odd_ref)
    build(0, even_ref)
    for block in range(blocks):
        if block + 1 < blocks:
            build(block + 1, buffers[(block + 1) % 2])
        multiply(block, buffers[block % 2])


def project(metric, recv, test, place, rows, edges=(), acc=(), send=False):
    groups, _, m, ny = recv.shape
    n = groups * m
    width = 2 * len(rows)
    args = [metric, recv, test, place, *edges, *acc]
    return pl.pallas_call(
        lambda *refs: kernel(*refs, rows=rows, edges=bool(edges), more=bool(acc), send=send),
        in_specs=[VMEM] * 3 + [SMEM] + [VMEM] * (len(args) - 4),
        out_specs=VMEM,
        out_shape=jax.ShapeDtypeStruct((n // 2, n // 2, 2 * n), jnp.float32),
        scratch_shapes=[
            pltpu.VMEM((2, width, n, ny), jnp.float32),
            pltpu.VMEM((width, n, ny), jnp.float32),
            pltpu.VMEM((n, width * ny), jnp.bfloat16),
            pltpu.VMEM((JB * n, width * ny), jnp.bfloat16),
            pltpu.VMEM((JB * n, width * ny), jnp.bfloat16),
        ],
        compiler_params=pltpu.CompilerParams(vmem_limit_bytes=LIMIT),
    )(*args)


def finish_kernel(shares_ref, out_ref, *, factor):
    count, _, width = shares_ref.shape
    total = sum(shares_ref[q].astype(jnp.float32) for q in range(count)) * factor
    out_ref[...] = jnp.concatenate([total[:, : width // 2], total[:, width // 2 :]], axis=0)


def finish(shares, factor):
    _, half, width = shares.shape
    return pl.pallas_call(
        lambda *refs: finish_kernel(*refs, factor=factor),
        in_specs=[VMEM],
        out_specs=VMEM,
        out_shape=jax.ShapeDtypeStruct((2 * half, width // 2), jnp.float32),
        compiler_params=pltpu.CompilerParams(vmem_limit_bytes=LIMIT),
        name="finish",
    )(shares)


def body(mode_fields, metric, plan):
    ny = mode_fields.shape[3]
    groups = lax.axis_size(MODE)
    place = lax.axis_index(MODE + ("c",)).astype(jnp.int32).reshape(1)
    plan = pltpu.with_memory_space_constraint(plan.T, pltpu.HBM)
    raw = pltpu.with_memory_space_constraint(mode_fields, pltpu.HBM)
    fields, packed, pick = pack(plan, place, raw, groups)
    pieces = lax.all_to_all(packed, MODE, 0, 0, tiled=True)
    recv = lax.all_to_all(choose(pick, pieces), MODE, 0, 0, tiled=True)
    count = lax.axis_size(SPACE)
    inner, outer = edge_rows(place, recv)
    between = [(i, i + 1 if i % 2 else i - 1) for i in range(1, count - 1)]
    outer = lax.ppermute(outer, SPACE, between)
    inner = lax.ppermute(inner, "c", [(0, 1), (1, 0)])
    edges = (inner, outer)
    middle = project(metric, recv, fields, place, (1, 2), send=True)
    sent = project(metric, recv, fields, place, (0, 3), edges, (middle,), send=True)
    other = lax.ppermute(sent, "c", [(0, 1), (1, 0)])
    kept = project(metric, recv, fields, place, (0, 1, 2, 3), edges)
    shares = lax.all_to_all((kept + other).astype(jnp.bfloat16), ("y", "zh"), 0, 0, tiled=True)
    return finish(shares, float(4 * count * ny) ** (-0.5))


def solution(mesh):
    fine = Mesh(mesh.devices.reshape(4, 2, 8, 4, 2), ("x", "zl", "y", "zh", "c"))
    return jax.shard_map(
        body,
        mesh=fine,
        in_specs=(P(MODE, None, SPACE, None), P(None, SPACE, None), P()),
        out_specs=P(SPACE, MODE),
        check_vma=False,
    )
```

```python
import jax
import jax.numpy as jnp
from jax import lax
from jax.experimental import pallas as pl
from jax.experimental.pallas import tpu as pltpu
from jax.sharding import Mesh, PartitionSpec as P


MODE = ("x", "zl")
RING = ("zl", "x")
SPACE = ("y", "zh", "c")
JB = 4
LIMIT = 16 * 2**20
SMEM = pl.BlockSpec(memory_space=pltpu.SMEM)
HBM = pl.BlockSpec(memory_space=pltpu.HBM)
VMEM = pl.BlockSpec(memory_space=pltpu.VMEM)


def pack_kernel(plan_hbm, place_ref, raw_hbm, fields_ref, out_ref, pick_ref, plan_ref, raw_ref, sems):
    raw_copy = pltpu.make_async_copy(raw_hbm, raw_ref, sems.at[0])
    plan_copy = pltpu.make_async_copy(plan_hbm, plan_ref, sems.at[1])
    raw_copy.start()
    plan_copy.start()
    raw_copy.wait()
    groups, _, m, _ = fields_ref.shape
    for g in range(groups):
        for c in range(2):
            block = raw_ref[g * m : (g + 1) * m, c].astype(jnp.float32)
            fields_ref[g, 4 * c : 4 * c + 4] = jnp.swapaxes(block, 0, 1).astype(fields_ref.dtype)
    plan_copy.wait()
    half = groups // 2
    for b in range(2):
        mover = plan_ref[1, b] * half
        moved = plan_ref[1, 2 + b] * half
        for g in range(half):
            out_ref[b * half + g, 0:8] = fields_ref[mover + g]
            out_ref[b * half + g, 8:16] = fields_ref[moved + g]
    block = place_ref[0] // groups
    for kind in range(2):
        owner = plan_ref[0, 2 * kind + block]
        owner = owner % 2 * half + owner // 2
        for g in range(groups):
            pick_ref[kind, g] = jnp.full(pick_ref.shape[2:], jnp.where(owner == g, 1.0, 0.0), pick_ref.dtype)


def pack(plan, place, mode_fields, groups):
    modes, _, _, ny = mode_fields.shape
    m = modes // groups
    return pl.pallas_call(
        pack_kernel,
        in_specs=[HBM, SMEM, HBM],
        out_specs=[VMEM, VMEM, VMEM],
        out_shape=[
            jax.ShapeDtypeStruct((groups, 8, m, ny), mode_fields.dtype),
            jax.ShapeDtypeStruct((groups, 16, m, ny), mode_fields.dtype),
            jax.ShapeDtypeStruct((2, groups, m, ny), jnp.float32),
        ],
        scratch_shapes=[
            pltpu.SMEM(plan.shape, plan.dtype),
            pltpu.VMEM(mode_fields.shape, mode_fields.dtype),
            pltpu.SemaphoreType.DMA((2,)),
        ],
        compiler_params=pltpu.CompilerParams(vmem_limit_bytes=LIMIT),
        name="pack",
    )(plan, place, mode_fields)


def choose_kernel(pick_ref, pieces_ref, out_ref):
    groups = pieces_ref.shape[0]
    for r in range(16):
        piece = sum(pieces_ref[g, r].astype(jnp.float32) * pick_ref[r // 8, g] for g in range(groups))
        for g in range(groups):
            out_ref[g, r] = piece.astype(out_ref.dtype)


def choose(pick, pieces):
    return pl.pallas_call(
        choose_kernel,
        in_specs=[VMEM, VMEM],
        out_specs=VMEM,
        out_shape=jax.ShapeDtypeStruct(pieces.shape, pieces.dtype),
        compiler_params=pltpu.CompilerParams(vmem_limit_bytes=LIMIT),
        name="choose",
    )(pick, pieces)


def edge_kernel(place_ref, recv_ref, inner_ref, outer_ref):
    core = place_ref[0] % 2
    for c in range(2):
        inner_ref[:, c] = recv_ref[:, 8 + 4 * c + 3 * (1 - core)]
        outer_ref[:, c] = recv_ref[:, 8 + 4 * c + 3 * core]


def edge_rows(place, recv):
    groups, _, m, ny = recv.shape
    shape = jax.ShapeDtypeStruct((groups, 2, m, ny), recv.dtype)
    return pl.pallas_call(
        edge_kernel,
        in_specs=[SMEM, VMEM],
        out_specs=[VMEM, VMEM],
        out_shape=[shape, shape],
        compiler_params=pltpu.CompilerParams(vmem_limit_bytes=LIMIT),
        name="edge_rows",
    )(place, recv)


def kernel(*refs, rows, edges, more, send):
    metric_ref, recv_ref, test_ref, place_ref, *refs = refs
    core = place_ref[0] % 2
    if edges:
        first = core == 0
        inner_ref, outer_ref, *refs = refs
    if more:
        acc_ref, *refs = refs
    out_ref, s_ref, wm_ref, phi_ref, even_ref, odd_ref = refs
    groups, _, m, ny = recv_ref.shape
    n = groups * m
    f32 = jnp.float32
    count = len(rows)

    def flat(block):
        return block.astype(f32).reshape(n, ny)

    def row(c, r):
        if r < 0:
            return jnp.where(first, flat(outer_ref[:, c]), flat(inner_ref[:, c]))
        if r > 3:
            return jnp.where(first, flat(inner_ref[:, c]), flat(outer_ref[:, c]))
        return flat(recv_ref[:, 8 + 4 * c + r])

    lane = lax.broadcasted_iota(jnp.int32, (n, ny), 1)
    for c in range(2):
        for i, r in enumerate(rows):
            at = count * c + i
            mid = row(c, r)
            along_x = (row(c, r + 1) - row(c, r - 1)) * metric_ref[0, pl.ds(r, 1), :]
            after = jnp.where(lane == ny - 1, 0.0, pltpu.roll(mid, ny - 1, 1))
            before = jnp.where(lane == 0, 0.0, pltpu.roll(mid, 1, 1))
            along_y = (after - before) * metric_ref[1, pl.ds(r, 1), :]
            s_ref[0, at] = along_x.astype(jnp.bfloat16).astype(f32)
            s_ref[1, at] = along_y.astype(jnp.bfloat16).astype(f32)
            wm_ref[at] = flat(recv_ref[:, 4 * c + r]) * metric_ref[2, pl.ds(r, 1), :]
            phi_ref[:, pl.ds(at * ny, ny)] = test_ref[:, 4 * c + r].reshape(n, ny)

    side = 1 - core if send else core

    def build(block, f_ref):
        for at in range(2 * count):
            i = at % count
            s0 = s_ref[0, at]
            s1 = s_ref[1, at]
            for b in range(JB):
                slot = block * JB + b
                j = pl.ds(2 * slot + side, 1)
                field = wm_ref[i, j, :] * s0 + wm_ref[count + i, j, :] * s1
                f_ref[pl.ds(b * n, n), pl.ds(at * ny, ny)] = field.astype(jnp.bfloat16)

    def multiply(block, f_ref):
        res = lax.dot_general(f_ref[...], phi_ref[...], (((1,), (1,)), ((), ())), preferred_element_type=f32)
        res = res.reshape(JB, n, n)
        res = jnp.concatenate([res[:, : n // 2], res[:, n // 2 :]], axis=2)
        here = pl.ds(block * JB, JB)
        if more:
            res = res + acc_ref[here]
        out_ref[here] = res.astype(out_ref.dtype)

    blocks = out_ref.shape[0] // JB
    buffers = (even_ref, odd_ref)
    build(0, even_ref)
    for block in range(blocks):
        if block + 1 < blocks:
            build(block + 1, buffers[(block + 1) % 2])
        multiply(block, buffers[block % 2])


def project(metric, recv, test, place, rows, edges=(), acc=(), send=False):
    groups, _, m, ny = recv.shape
    n = groups * m
    width = 2 * len(rows)
    args = [metric, recv, test, place, *edges, *acc]
    return pl.pallas_call(
        lambda *refs: kernel(*refs, rows=rows, edges=bool(edges), more=bool(acc), send=send),
        in_specs=[VMEM] * 3 + [SMEM] + [VMEM] * (len(args) - 4),
        out_specs=VMEM,
        out_shape=jax.ShapeDtypeStruct((n // 2, n // 2, 2 * n), jnp.float32),
        scratch_shapes=[
            pltpu.VMEM((2, width, n, ny), jnp.float32),
            pltpu.VMEM((width, n, ny), jnp.float32),
            pltpu.VMEM((n, width * ny), jnp.bfloat16),
            pltpu.VMEM((JB * n, width * ny), jnp.bfloat16),
            pltpu.VMEM((JB * n, width * ny), jnp.bfloat16),
        ],
        compiler_params=pltpu.CompilerParams(vmem_limit_bytes=LIMIT),
    )(*args)


def finish_kernel(shares_ref, out_ref, *, factor):
    count, _, width = shares_ref.shape
    total = sum(shares_ref[q].astype(jnp.float32) for q in range(count)) * factor
    out_ref[...] = jnp.concatenate([total[:, : width // 2], total[:, width // 2 :]], axis=0)


def finish(shares, factor):
    _, half, width = shares.shape
    return pl.pallas_call(
        lambda *refs: finish_kernel(*refs, factor=factor),
        in_specs=[VMEM],
        out_specs=VMEM,
        out_shape=jax.ShapeDtypeStruct((2 * half, width // 2), jnp.float32),
        compiler_params=pltpu.CompilerParams(vmem_limit_bytes=LIMIT),
        name="finish",
    )(shares)


def body(mode_fields, metric, plan):
    ny = mode_fields.shape[3]
    groups = lax.axis_size(RING)
    place = lax.axis_index(RING + ("c",)).astype(jnp.int32).reshape(1)
    plan = pltpu.with_memory_space_constraint(plan.T, pltpu.HBM)
    raw = pltpu.with_memory_space_constraint(mode_fields, pltpu.HBM)
    fields, packed, pick = pack(plan, place, raw, groups)
    pieces = lax.all_to_all(packed, RING, 0, 0, tiled=True)
    recv = lax.all_to_all(choose(pick, pieces), RING, 0, 0, tiled=True)
    count = lax.axis_size(SPACE)
    inner, outer = edge_rows(place, recv)
    between = [(i, i + 1 if i % 2 else i - 1) for i in range(1, count - 1)]
    outer = lax.ppermute(outer, SPACE, between)
    middle = project(metric, recv, fields, place, (1, 2), send=True)
    inner, middle = lax.optimization_barrier((inner, middle))
    inner = lax.ppermute(inner, "c", [(0, 1), (1, 0)])
    edges = (inner, outer)
    sent = project(metric, recv, fields, place, (0, 3), edges, (middle,), send=True)
    other = lax.ppermute(sent, "c", [(0, 1), (1, 0)])
    kept = project(metric, recv, fields, place, (0, 1, 2, 3), edges)
    shares = lax.all_to_all((kept + other).astype(jnp.bfloat16), ("y", "zh"), 0, 0, tiled=True)
    return finish(shares, float(4 * count * ny) ** (-0.5))


def solution(mesh):
    fine = Mesh(mesh.devices.reshape(4, 2, 8, 4, 2), ("x", "zl", "y", "zh", "c"))
    return jax.shard_map(
        body,
        mesh=fine,
        in_specs=(P(MODE, None, SPACE, None), P(None, SPACE, None), P()),
        out_specs=P(SPACE, MODE),
        check_vma=False,
    )
```
